32 devices in a mesh: heads: 4 (over y, core), tok: 8 (over z, x).
Axes of the slice: x: 2, y: 2, z: 4, core: 2. Of those that a mesh axis runs over, the one named last changes fastest.
Arguments:
- video_q: bfloat16 [8192, 2048], P('tok', 'heads'), as said below
- video_k: bfloat16 [8192, 2048], P('tok', 'heads'), as said below
- video_v: bfloat16 [8192, 2048], P('tok', 'heads'), may hold values from -6 to 6
- audio_q: bfloat16 [512, 2048], P('tok', 'heads'), as said below
- audio_k: bfloat16 [512, 2048], P('tok', 'heads'), as said below
- audio_v: bfloat16 [512, 2048], P('tok', 'heads'), may hold values from -6 to 6
- video_q_gain: float32 [2048], P('heads'), may hold values from 0.1 to 1.9
- audio_k_gain: float32 [2048], P('heads'), may hold values from 0.1 to 1.9
- audio_q_gain: float32 [2048], P('heads'), may hold values from 0.1 to 1.9
- video_k_gain: float32 [2048], P('heads'), may hold values from 0.1 to 1.9
Outputs:
- video_out: bfloat16 [8192, 2048], P('tok', 'heads')
- audio_out: bfloat16 [512, 2048], P('tok', 'heads')
The draws below stay inside these ranges and needn't reach their ends.
Inputs may be any that keep to these rules, and one draw needn't show every extreme that they name: `video_q`: no row is zero. `video_k`: no row is zero. `audio_q`: no row is zero. `audio_k`: no row is zero.
All inputs are finite; a program needn't handle non-finite values.
Results may differ from the reference program's by a relative error of at most 0.012.
The reference program's roundings to bfloat16 on the way count: a program that leaves them out, or rounds other values in their place, can miss the bound.
Values may be sent and summed in bfloat16 or wider, within the bound.
No kernel may reach another device: no remote copies, remote signals or barrier semaphores. Data moves between devices by JAX's collectives and lax.ppermute only.
A program may use at most 64 MiB of HBM per device.

```python
import math
import jax
import jax.numpy as jnp
from jax import lax

HEADS = 32
HD = 64
TOK_V = 1024
WIDTH = 2048
TOKENS = 8192
AUDIO = 512
N_TOK = 8


def texture(key, count):
    first_key, second_key, third_key = jax.random.split(key, 3)
    base = jax.random.normal(first_key, (count, WIDTH), jnp.float32)
    column = jnp.exp(jnp.log(3.0) * jnp.arange(WIDTH, dtype=jnp.float32) / (WIDTH - 1))
    column = column * jnp.exp(jax.random.uniform(second_key, (WIDTH,), jnp.float32) * jnp.log(2.5))
    row_scale = jnp.exp(jax.random.uniform(third_key, (count, 1), jnp.float32) * jnp.log(10.0))
    return base * column * row_scale


def beacons(key):
    shared = jax.random.fold_in(key, 4242)
    first_key, second_key, third_key = jax.random.split(shared, 3)
    index = jnp.arange(4)
    owner = index * HEADS // 4
    heads_of = jnp.arange(WIDTH) // HD
    inside = (heads_of[None, :] == owner[:, None]).astype(jnp.float32)
    strength = 0.03 * (index.astype(jnp.float32)[:, None] + 1.0)
    direction = jax.random.normal(first_key, (4, WIDTH), jnp.float32)
    background = jax.random.normal(second_key, (4, WIDTH), jnp.float32) * strength
    vectors = inside * direction + (1.0 - inside) * background
    nudge = (1.0 - inside) * 0.02 * jax.random.normal(third_key, (4, WIDTH), jnp.float32)
    return (vectors, vectors + nudge)


def draw_video_q(key, part):
    values = texture(jax.random.fold_in(key, 11), TOKENS)
    vectors, nudged = beacons(key)
    values = values.at[jnp.arange(4) * (TOKENS // 4) + 5].set(vectors)
    return values.astype(jnp.bfloat16)


def draw_audio_k(key, part):
    values = texture(jax.random.fold_in(key, 12), AUDIO)
    vectors, nudged = beacons(key)
    values = values.at[jnp.arange(4) * (AUDIO // 4) + 1].set(vectors)
    values = values.at[jnp.arange(4) * (AUDIO // 4) + 2].set(nudged)
    return values.astype(jnp.bfloat16)


def draw_audio_q(key, part):
    values = texture(jax.random.fold_in(key, 13), AUDIO)
    vectors, nudged = beacons(key)
    values = values.at[jnp.arange(4) * (AUDIO // 4) + 3].set(vectors)
    return values.astype(jnp.bfloat16)


def draw_video_k(key, part):
    values = texture(jax.random.fold_in(key, 14), TOKENS)
    vectors, nudged = beacons(key)
    values = values.at[jnp.arange(4) * (TOKENS // 4) + 7].set(vectors)
    values = values.at[jnp.arange(4) * (TOKENS // 4) + 8].set(nudged)
    return values.astype(jnp.bfloat16)


def level_of(stream_key, extent, shards, least, high):
    level = 1.0
    for axis_at, blocks in shards:
        steps = jax.random.uniform(jax.random.fold_in(jax.random.fold_in(stream_key, 6), axis_at), (blocks,), jnp.float32, least / len(shards), high / len(shards))
        level = level * jnp.repeat(jnp.exp(steps), extent[axis_at] // blocks).reshape((-1,) + (1,) * (len(extent) - 1 - axis_at))
    return level


def gaussian(key, extent, width, bound, shards=(), held_as=jnp.bfloat16):
    entries = jax.random.normal(key, extent, jnp.float32) * width
    if len(shards) > 0:
        entries = level_of(key, extent, shards, -0.22, 0.18) * entries
    return jnp.clip(entries, min=-bound, max=bound).astype(held_as)


def setup_inputs(seed: int = 0) -> dict:
    arg_keys = jax.random.split(jax.random.key(seed), 11)
    return {
        "video_q": draw_video_q(jax.random.fold_in(arg_keys[10], 71), 0),
        "video_k": draw_video_k(jax.random.fold_in(arg_keys[10], 71), 0),
        "video_v": gaussian(arg_keys[2], (TOKENS, WIDTH), 1.0, 6.0, ((0, 8), (1, 4))),
        "audio_q": draw_audio_q(jax.random.fold_in(arg_keys[10], 71), 0),
        "audio_k": draw_audio_k(jax.random.fold_in(arg_keys[10], 71), 0),
        "audio_v": gaussian(arg_keys[5], (AUDIO, WIDTH), 1.0, 6.0, ((0, 8), (1, 4))),
        "video_q_gain": jnp.clip(1.0 + 0.18 * jax.random.normal(arg_keys[6], (WIDTH,), jnp.float32), 0.1, 1.9),
        "audio_k_gain": jnp.clip(1.0 + 0.18 * jax.random.normal(arg_keys[7], (WIDTH,), jnp.float32), 0.1, 1.9),
        "audio_q_gain": jnp.clip(1.0 + 0.18 * jax.random.normal(arg_keys[8], (WIDTH,), jnp.float32), 0.1, 1.9),
        "video_k_gain": jnp.clip(1.0 + 0.18 * jax.random.normal(arg_keys[9], (WIDTH,), jnp.float32), 0.1, 1.9),
    }


EPS = 1e-06

def normalize(rows, gain):
    values = rows.astype(jnp.float32)
    mean_sq = lax.optimization_barrier(jnp.mean(values * values, axis=1, keepdims=True))
    return (values * lax.rsqrt(mean_sq + EPS) * gain.astype(jnp.float32)).astype(jnp.bfloat16)

def reference(video_q, video_k, video_v, audio_q, audio_k, audio_v, video_q_gain, audio_k_gain, audio_q_gain, video_k_gain):
    factor = HD ** (-0.5)
    query_v = normalize(video_q, video_q_gain)
    key_a = normalize(audio_k, audio_k_gain).reshape(AUDIO, HEADS, HD).astype(jnp.float32)
    query_a = normalize(audio_q, audio_q_gain).reshape(AUDIO, HEADS, HD).astype(jnp.float32)
    key_v = normalize(video_k, video_k_gain)
    value_a = audio_v.reshape(AUDIO, HEADS, HD).astype(jnp.float32)
    block = math.gcd(TOKENS, 512)
    count = TOKENS // block

    def first(pair):
        query, value = pair
        scores = jnp.einsum('qhd,khd->hqk', query.reshape(block, HEADS, HD).astype(jnp.float32), key_a) * factor
        top = lax.optimization_barrier(jnp.max(scores, axis=-1, keepdims=True))
        expo = jnp.exp(scores - top)
        total = lax.optimization_barrier(jnp.sum(expo, axis=-1))
        weights = lax.optimization_barrier(expo.astype(jnp.bfloat16)).astype(jnp.float32)
        mixed = jnp.einsum('hqk,khd->qhd', weights, value_a) / jnp.transpose(total)[:, :, None]
        return (value.astype(jnp.float32) + mixed.reshape(block, WIDTH)).astype(jnp.bfloat16)
    video_out = lax.map(first, (query_v.reshape(count, block, WIDTH), video_v.reshape(count, block, WIDTH))).reshape(TOKENS, WIDTH)
    key_blocks = key_v.reshape(N_TOK, TOK_V, HEADS, HD)
    value_blocks = video_out.reshape(N_TOK, TOK_V, HEADS, HD)

    def second(carry, pair):
        run_top, run_out, run_total = carry
        keys, values = pair
        scores = jnp.einsum('qhd,khd->hqk', query_a, keys.astype(jnp.float32)) * factor
        top = lax.optimization_barrier(jnp.max(scores, axis=-1))
        expo = jnp.exp(scores - top[:, :, None])
        total = lax.optimization_barrier(jnp.sum(expo, axis=-1))
        weights = lax.optimization_barrier(expo.astype(jnp.bfloat16)).astype(jnp.float32)
        part = jnp.einsum('hqk,khd->hqd', weights, values.astype(jnp.float32))
        new_top = jnp.maximum(run_top, top)
        old_f = jnp.exp(run_top - new_top)
        new_f = jnp.exp(top - new_top)
        run_out = run_out * old_f[:, :, None] + part * new_f[:, :, None]
        run_total = run_total * old_f + total * new_f
        return ((new_top, run_out, run_total), None)
    start = (jnp.full((HEADS, AUDIO), -1e+30, jnp.float32), jnp.zeros((HEADS, AUDIO, HD), jnp.float32), jnp.zeros((HEADS, AUDIO), jnp.float32))
    (last_top, summed, totals), unused = lax.scan(second, start, (key_blocks, value_blocks))
    result = summed / totals[:, :, None]
    audio_out = jnp.transpose(result, (1, 0, 2)).reshape(AUDIO, WIDTH).astype(jnp.bfloat16)
    return (video_out, audio_out)
```

```python
import math

import jax
import jax.numpy as jnp
from jax import lax
from jax.experimental import pallas as pl
from jax.experimental.pallas import tpu as pltpu
from jax.sharding import PartitionSpec as P

HEADS = 32
HD = 64
EPS = 1e-06
LANES = 2 * HD
SLOT = 16
FACTOR = HD ** (-0.5)
BASE2 = FACTOR * math.log2(math.e)

BF16 = jnp.bfloat16
F32 = jnp.float32


def squares(rows):
    values = rows.astype(F32)
    return jnp.sum(values * values, axis=1)


def normalize(rows, summed, gain):
    scaled = lax.rsqrt(summed / (HEADS * HD) + EPS)[:, None]
    return (rows.astype(F32) * scaled * gain).astype(BF16)


def partner(value, axis, size, bit):
    return lax.ppermute(value, axis, [(i, i ^ bit) for i in range(size)])


def low_lanes():
    return lax.broadcasted_iota(jnp.int32, (1, LANES), 1) < HD


def with_ones(low, values):
    one = jnp.ones_like(values)
    return jnp.where(low, values, one), jnp.where(low, one, values)


def pair_scores(low, query, keys):
    zero = jnp.zeros_like(query)
    for part in (jnp.where(low, query, zero), jnp.where(low, zero, query)):
        yield lax.dot_general(part, keys, (((1,), (1,)), ((), ())), preferred_element_type=F32)


def weights_of(scores):
    top = jnp.max(scores, axis=1, keepdims=True)
    return top, jnp.exp2((scores - top) * BASE2).astype(BF16)


def first_kernel(count, query_ref, value_ref, *refs):
    key_refs, mix_refs = refs[:count], refs[count : 2 * count]
    out_ref, keys, mixes = refs[2 * count :]
    width = query_ref.shape[1]
    low = low_lanes()

    @pl.when(pl.program_id(0) == 0)
    def _():
        at = 0
        for key_ref, mix_ref in zip(key_refs, mix_refs):
            rows = pl.ds(at, key_ref.shape[0])
            keys[rows, :] = key_ref[...]
            for p in range(width // LANES):
                left, right = with_ones(low, mix_ref[:, p * LANES : (p + 1) * LANES])
                mixes[2 * p, rows, :] = left
                mixes[2 * p + 1, rows, :] = right
            at += key_ref.shape[0]

    for p in range(width // LANES):
        cols = slice(p * LANES, (p + 1) * LANES)
        got = []
        for half, scores in enumerate(pair_scores(low, query_ref[:, cols], keys[:, cols])):
            _, weights = weights_of(scores)
            got.append(jnp.dot(weights, mixes[2 * p + half], preferred_element_type=F32))
        mixed = jnp.where(low, got[0], got[1])
        total = pltpu.roll(jnp.where(low, got[1], got[0]), HD, 1)
        out_ref[:, cols] = (value_ref[:, cols].astype(F32) + mixed / total).astype(BF16)


def first_attention(query, value, keys, mixes):
    rows, width = query.shape
    block = math.gcd(rows, 512)
    total = sum(k.shape[0] for k in keys)
    tile = pl.BlockSpec((block, width), lambda i: (i, 0))
    whole = [pl.BlockSpec(k.shape, lambda i: (0, 0)) for k in keys]
    return pl.pallas_call(
        lambda *refs: first_kernel(len(keys), *refs),
        grid=(rows // block,),
        in_specs=[tile, tile] + whole + whole,
        out_specs=tile,
        out_shape=jax.ShapeDtypeStruct((rows, width), BF16),
        scratch_shapes=[
            pltpu.VMEM((total, width), BF16),
            pltpu.VMEM((width // HD, total, LANES), BF16),
        ],
        compiler_params=pltpu.CompilerParams(dimension_semantics=("arbitrary",)),
    )(query, value, *keys, *mixes)


def three(values):
    parts = []
    for _ in range(3):
        parts.append(values.astype(BF16))
        values = values - parts[-1].astype(F32)
    return parts


def second_kernel(count, *refs):
    query_refs, (key_ref, value_ref) = refs[:count], refs[count : count + 2]
    out_refs, queries = refs[count + 2 : 2 * count + 2], refs[2 * count + 2]
    width = key_ref.shape[1]
    rows = query_refs[0].shape[0]
    lane = lax.broadcasted_iota(jnp.int32, (1, LANES), 1)
    low = low_lanes()
    for c, query_ref in enumerate(query_refs):
        queries[pl.ds(c * rows, rows), :] = query_ref[...]
    tops = totals = jnp.zeros((1, LANES), F32)
    for p in range(width // LANES):
        cols = slice(p * LANES, (p + 1) * LANES)
        got, top = [], []
        pairs = pair_scores(low, queries[:, cols], key_ref[:, cols])
        for scores, mix in zip(pairs, with_ones(low, value_ref[:, cols])):
            highest, weights = weights_of(scores)
            top.append(highest)
            got.append(jnp.dot(weights, mix, preferred_element_type=F32))
        mixed = jnp.where(low, got[0], got[1]).astype(BF16)
        for c in range(count):
            out_refs[c][:, cols] = mixed[c * rows : (c + 1) * rows]
        here = (lane % HD) // SLOT == p
        tops = jnp.where(here, jnp.where(low, top[0], top[1]), tops)
        totals = jnp.where(here, jnp.where(low, got[1], got[0]), totals)
    stats = jnp.zeros(tops.shape, BF16)
    for i, part in enumerate(three(totals) + three(tops)):
        stats = jnp.where(lane % SLOT == i, part, stats)
    for c in range(count):
        out_refs[c][:, width:] = stats[c * rows : (c + 1) * rows]


def second_attention(queries, keys, values):
    width = keys.shape[1]
    rows = sum(q.shape[0] for q in queries)
    return pl.pallas_call(
        lambda *refs: second_kernel(len(queries), *refs),
        out_shape=tuple(
            jax.ShapeDtypeStruct((q.shape[0], width + LANES), BF16) for q in queries
        ),
        scratch_shapes=[pltpu.VMEM((rows, width), BF16)],
    )(*queries, keys, values)


def combine_kernel(*refs):
    part_refs, out_ref = refs[:-1], refs[-1]
    width = out_ref.shape[1]
    row = lax.broadcasted_iota(jnp.int32, (LANES, width), 0)
    col = lax.broadcasted_iota(jnp.int32, (LANES, width), 1)
    half = (col % LANES) // HD
    mine = (row % HD) // SLOT == col // LANES
    kind = row % SLOT
    pick_total = (mine & (row // HD == 1 - half) & (kind < 3)).astype(F32).astype(BF16)
    pick_top = (mine & (row // HD == half) & (kind >= 3) & (kind < 6)).astype(F32).astype(BF16)
    totals, tops = [], []
    for ref in part_refs:
        stats = ref[:, width:]
        totals.append(jnp.dot(stats, pick_total, preferred_element_type=F32))
        tops.append(jnp.dot(stats, pick_top, preferred_element_type=F32))
    highest = tops[0]
    for top in tops[1:]:
        highest = jnp.maximum(highest, top)
    summed = denominator = 0.0
    for ref, total, top in zip(part_refs, totals, tops):
        scale = jnp.exp2((top - highest) * BASE2)
        summed = summed + ref[:, :width].astype(F32) * scale
        denominator = denominator + total * scale
    out_ref[...] = (summed / denominator).astype(BF16)


def combine(parts):
    rows, wide = parts[0].shape
    return pl.pallas_call(
        combine_kernel,
        out_shape=jax.ShapeDtypeStruct((rows, wide - LANES), BF16),
    )(*parts)


def gather(own, size):
    even = {0: own}
    for bit in range(2, size, 2):
        even[bit] = partner(own, "tok", size, bit)
    chunks = []
    for bit in range(0, size, 2):
        chunks += [even[bit], partner(even[bit], "tok", size, 1)]
    return chunks


def body_of(n_heads, n_tok):
    def body(
        video_q,
        video_k,
        video_v,
        audio_q,
        audio_k,
        audio_v,
        video_q_gain,
        audio_k_gain,
        audio_q_gain,
        video_k_gain,
    ):
        tok_rows = video_q.shape[0]
        aud_rows = audio_q.shape[0]
        mine = jnp.concatenate(
            [squares(audio_k), squares(audio_q), squares(video_q), squares(video_k)]
        )
        summed = mine
        for bit in range(1, n_heads):
            summed = summed + partner(mine, "heads", n_heads, bit)
        sum_ak, sum_aq = summed[:aud_rows], summed[aud_rows : 2 * aud_rows]
        sum_vq = summed[2 * aud_rows : 2 * aud_rows + tok_rows]
        sum_vk = summed[2 * aud_rows + tok_rows :]
        mixes = gather(audio_v, n_tok)
        keys = gather(normalize(audio_k, sum_ak, audio_k_gain), n_tok)
        queries = gather(normalize(audio_q, sum_aq, audio_q_gain), n_tok)
        query_v = normalize(video_q, sum_vq, video_q_gain)
        key_v = normalize(video_k, sum_vk, video_k_gain)
        video_out = first_attention(query_v, video_v, keys, mixes)
        step = max(1, 512 // aud_rows)
        parts = []
        for at in range(0, n_tok, step):
            parts += second_attention(queries[at : at + step], key_v, video_out)
        got = [parts[0]] + [partner(parts[j], "tok", n_tok, j) for j in range(1, n_tok)]
        return (video_out, combine(got))

    return body


def solution(mesh):
    return jax.shard_map(
        body_of(mesh.shape["heads"], mesh.shape["tok"]),
        mesh=mesh,
        in_specs=(P("tok", "heads"),) * 6 + (P("heads"),) * 4,
        out_specs=(P("tok", "heads"), P("tok", "heads")),
        check_vma=False,
    )
```
